32 devices in a mesh: freq: 4 (over y, x), trace: 8 (over z, core).
Axes of the slice: x: 2, y: 2, z: 4, core: 2. Of those that a mesh axis runs over, the one named last changes fastest.
Arguments:
- traces: float32 [64, 256, 2048], P(('freq', 'trace')), may hold values from -6 to 6
- source_weights: float32 [64, 256, 512], P(None, 'trace'), may hold values from -0.09375 to 0.09375
- level_weights: float32 [3, 2048, 1024], P(None, 'trace'), may hold values from -0.1875 to 0.1875
- slowness_weights: float32 [4096, 512], P('trace'), may hold values from -0.25 to 0.25
Outputs:
- radon_image: float32 [4096, 256], P(('trace', 'freq'))
The draws below stay inside these ranges and needn't reach their ends.
All inputs are finite; a program needn't handle non-finite values.
Results may differ from the reference program's by a relative error of at most 0.00011.
Values sent between devices are 32-bit elements; how exact they have to be, the bound alone decides.
A program may use at most 128 MiB of HBM per device.

```python
import math
import jax
import jax.numpy as jnp
import numpy as np
from jax import lax

SAMPLES = 2048
FREQS = 1024
OFFSETS = 256
K = 256
SLOW = 4096
TAUS = 256
SHOTS = 64
BOXES = 8
LEVELS = 3


def steps_of(own_key, dims, cuts, smallest, largest):
    factor_of, own = 1.0, jax.random.fold_in(own_key, 6)
    for dim, shards_of in cuts:
        draws = jnp.exp(jax.random.uniform(jax.random.fold_in(own, dim), (shards_of,), jnp.float32, smallest / len(cuts), largest / len(cuts)))
        factor_of = factor_of * jnp.repeat(draws, dims[dim] // shards_of).reshape([-1 if axis == dim else 1 for axis in range(len(dims))])
    return factor_of


def gaussian(stream_key, extent, deviation, bound, shards=(), kind=jnp.bfloat16):
    entries = jax.random.normal(stream_key, extent, jnp.float32) * deviation
    if len(shards) > 0:
        entries = steps_of(stream_key, extent, shards, -0.22, 0.18) * entries
    return jnp.clip(entries, min=-bound, max=bound).astype(kind)


def setup_inputs(seed: int = 0) -> dict:
    key_list = jax.random.split(jax.random.key(seed), 5)
    return {
        "traces": gaussian(key_list[0], (SHOTS, OFFSETS, SAMPLES), 1.0, 6.0, ((0, 32),), jnp.float32),
        "source_weights": gaussian(key_list[1], (SHOTS, OFFSETS, 2 * K), (2 * SHOTS * OFFSETS // BOXES) ** -0.5, 0.09375, ((1, 8),), jnp.float32),
        "level_weights": gaussian(key_list[2], (LEVELS, BOXES * K, 4 * K), (4 * K) ** -0.5, 0.1875, ((1, 8),), jnp.float32),
        "slowness_weights": gaussian(key_list[3], (SLOW, 2 * K), (2 * K) ** -0.5, 0.25, ((0, 8),), jnp.float32),
    }


def contract_box(weights, values):
    return jnp.einsum('sbok,sbof->bkf', weights, values, precision=lax.Precision.HIGHEST)

def apply_box(weights, values):
    return jnp.einsum('bkj,bjf->bkf', weights, values, precision=lax.Precision.HIGHEST)

def reference(traces, source_weights, level_weights, slowness_weights):
    spectrum = jnp.fft.rfft(traces, axis=-1)[..., :FREQS] / math.sqrt(SAMPLES)
    box_offsets = OFFSETS // BOXES
    spec_real = jnp.real(spectrum).astype(jnp.float32).reshape(SHOTS, BOXES, box_offsets, FREQS)
    spec_imag = jnp.imag(spectrum).astype(jnp.float32).reshape(SHOTS, BOXES, box_offsets, FREQS)
    sources = source_weights.reshape(SHOTS, BOXES, box_offsets, 2 * K)
    src_real = sources[..., :K]
    src_imag = sources[..., K:]
    coeff_real = contract_box(src_real, spec_real) - contract_box(src_imag, spec_imag)
    coeff_imag = contract_box(src_real, spec_imag) + contract_box(src_imag, spec_real)
    weights_all = level_weights.reshape(LEVELS, BOXES, K, 4 * K)
    box_ids = np.arange(BOXES)
    for level_no in range(LEVELS):
        partner = box_ids ^ 1 << level_no
        part_real = coeff_real[partner]
        part_imag = coeff_imag[partner]
        weights = weights_all[level_no]
        own_real = weights[..., :K]
        par_real = weights[..., K:2 * K]
        own_imag = weights[..., 2 * K:3 * K]
        par_imag = weights[..., 3 * K:]
        new_real = apply_box(own_real, coeff_real) - apply_box(own_imag, coeff_imag) + apply_box(par_real, part_real) - apply_box(par_imag, part_imag)
        new_imag = apply_box(own_real, coeff_imag) + apply_box(own_imag, coeff_real) + apply_box(par_real, part_imag) + apply_box(par_imag, part_real)
        coeff_real, coeff_imag = (new_real, new_imag)
    evaluate = slowness_weights.reshape(BOXES, SLOW // BOXES, 2 * K)
    eval_real = evaluate[..., :K]
    eval_imag = evaluate[..., K:]
    image_real = apply_box(eval_real, coeff_real) - apply_box(eval_imag, coeff_imag)
    image_imag = apply_box(eval_real, coeff_imag) + apply_box(eval_imag, coeff_real)
    tau_ids = jnp.arange(TAUS, dtype=jnp.int32) * (SAMPLES // (4 * TAUS))
    freq_ids = jnp.arange(FREQS, dtype=jnp.int32)
    turns = (freq_ids[:, None] * tau_ids[None, :] % SAMPLES).astype(jnp.float32) * (2.0 * math.pi / SAMPLES)
    cosines = jnp.cos(turns)
    sines = jnp.sin(turns)
    radon_image = (jnp.einsum('bpf,ft->bpt', image_real, cosines, precision=lax.Precision.HIGHEST) - jnp.einsum('bpf,ft->bpt', image_imag, sines, precision=lax.Precision.HIGHEST)) / math.sqrt(FREQS)
    return radon_image.reshape(SLOW, TAUS)
```

```python
import math

import jax
import jax.numpy as jnp
import numpy as np
from jax import lax
from jax.sharding import PartitionSpec as P

FREQS = 1024
TAUS = 256


SPLIT = lax.Precision.HIGH


def from_partner(block, axis, apart):
    count = lax.axis_size(axis)
    route = []
    for low in range(count):
        high = low | 1 << apart
        if high != low and high < count:
            route += [(low, high), (high, low)]
    return lax.ppermute(block, axis, route)


def product(left, right):
    return jnp.dot(left, right, precision=SPLIT, preferred_element_type=jnp.float32)


def lag_series(sample_count):
    lags = np.arange(sample_count)
    turns = (np.arange(FREQS)[:, None] * lags[None, :]) % sample_count
    return np.exp(2j * np.pi * turns / sample_count).sum(axis=0)


def imag_table(sample_count):
    series = lag_series(sample_count).imag
    step = sample_count // (4 * TAUS)
    lags = (np.arange(TAUS)[None, :] * step - np.arange(sample_count)[:, None]) % sample_count
    return (series[lags] / math.sqrt(sample_count * FREQS)).astype(np.float32)


def body(traces, source_weights, level_weights, slowness_weights):
    freq_count = lax.axis_size("freq")
    trace_count = lax.axis_size("trace")
    shot_dev, offset_count, sample_count = traces.shape
    tau_dev = TAUS // freq_count
    box_offsets = offset_count // trace_count
    coeff_count = source_weights.shape[2] // 2
    step = sample_count // (4 * TAUS)
    norm = 1.0 / math.sqrt(sample_count * FREQS)
    samples = traces.reshape(-1, sample_count)
    odd = (jnp.arange(sample_count) % 2 == 1).astype(jnp.float32)
    odd_sum = jnp.sum(samples * odd, axis=1, keepdims=True) * norm
    span = TAUS * step
    pick = (jnp.arange(span)[:, None] == jnp.arange(TAUS)[None, :] * step).astype(jnp.float32)
    folded_real = product(samples[:, :span], pick) * (FREQS * norm) + odd_sum
    folded_imag = product(samples, jnp.asarray(imag_table(sample_count)))
    folded_real = folded_real.reshape(shot_dev, trace_count, box_offsets, freq_count, 1, tau_dev)
    folded_imag = folded_imag.reshape(shot_dev, trace_count, box_offsets, freq_count, 1, tau_dev)
    folded = jnp.concatenate([folded_real, folded_imag], axis=4).reshape(
        shot_dev, trace_count, box_offsets, freq_count, 2 * tau_dev
    )
    folded = jnp.transpose(folded, (3, 1, 0, 2, 4)).reshape(
        freq_count * trace_count, shot_dev * box_offsets, 2 * tau_dev
    )
    folded = lax.all_to_all(folded, ("freq", "trace"), split_axis=0, concat_axis=0, tiled=True)
    folded = folded.reshape(-1, 2 * tau_dev)
    sources = source_weights.reshape(-1, 2 * coeff_count)
    gram = jnp.einsum(
        "xk,xc->kc", sources, folded, precision=SPLIT, preferred_element_type=jnp.float32
    )
    coeff_real = gram[:coeff_count, :tau_dev] - gram[coeff_count:, tau_dev:]
    coeff_imag = gram[:coeff_count, tau_dev:] + gram[coeff_count:, :tau_dev]
    coeffs = jnp.concatenate([coeff_real, coeff_imag], axis=1)
    for level_no in range(level_weights.shape[0]):
        partner = from_partner(coeffs, "trace", level_no)
        weights = level_weights[level_no]
        stacked = jnp.concatenate([coeffs, partner], axis=0)
        real_rows = product(weights[:, : 2 * coeff_count], stacked)
        imag_rows = product(weights[:, 2 * coeff_count :], stacked)
        coeffs = jnp.concatenate(
            [
                real_rows[:, :tau_dev] - imag_rows[:, tau_dev:],
                real_rows[:, tau_dev:] + imag_rows[:, :tau_dev],
            ],
            axis=1,
        )
    image = product(slowness_weights[:, :coeff_count], coeffs[:, :tau_dev]) - product(
        slowness_weights[:, coeff_count:], coeffs[:, tau_dev:]
    )
    return lax.all_to_all(image, "freq", split_axis=0, concat_axis=1, tiled=True)


def solution(mesh):
    return jax.shard_map(
        body,
        mesh=mesh,
        in_specs=(
            P(("freq", "trace"), None, None),
            P(None, "trace", None),
            P(None, "trace", None),
            P("trace", None),
        ),
        out_specs=P(("trace", "freq"), None),
        check_vma=False,
    )
```

```python
import functools
import math

import jax
import jax.numpy as jnp
import numpy as np
from jax import lax
from jax.experimental import pallas as pl
from jax.experimental.pallas import tpu as pltpu
from jax.sharding import PartitionSpec as P

FREQS = 1024
TAUS = 256


SPLIT = lax.Precision.HIGH


def from_partner(block, axis, apart):
    count = lax.axis_size(axis)
    route = []
    for low in range(count):
        high = low | 1 << apart
        if high != low and high < count:
            route += [(low, high), (high, low)]
    return lax.ppermute(block, axis, route)


def product(left, right):
    return jnp.dot(left, right, precision=SPLIT, preferred_element_type=jnp.float32)


def lag_series(sample_count):
    lags = np.arange(sample_count)
    turns = (np.arange(FREQS)[:, None] * lags[None, :]) % sample_count
    return np.exp(2j * np.pi * turns / sample_count).sum(axis=0)


def imag_table(sample_count):
    series = lag_series(sample_count).imag
    step = sample_count // (4 * TAUS)
    lags = (np.arange(TAUS)[None, :] * step - np.arange(sample_count)[:, None]) % sample_count
    return (series[lags] / math.sqrt(sample_count * FREQS)).astype(np.float32)


def body(traces, source_weights, level_weights, slowness_weights):
    freq_count = lax.axis_size("freq")
    trace_count = lax.axis_size("trace")
    shot_dev, offset_count, sample_count = traces.shape
    tau_dev = TAUS // freq_count
    box_offsets = offset_count // trace_count
    coeff_count = source_weights.shape[2] // 2
    step = sample_count // (4 * TAUS)
    norm = 1.0 / math.sqrt(sample_count * FREQS)
    samples = traces.reshape(-1, sample_count)
    odd = (jnp.arange(sample_count) % 2 == 1).astype(jnp.float32)
    odd_sum = jnp.sum(samples * odd, axis=1, keepdims=True) * norm
    span = TAUS * step
    pick = (jnp.arange(span)[:, None] == jnp.arange(TAUS)[None, :] * step).astype(jnp.float32)
    folded_real = product(samples[:, :span], pick) * (FREQS * norm) + odd_sum
    folded_imag = product(samples, jnp.asarray(imag_table(sample_count)))
    folded_real = folded_real.reshape(shot_dev, trace_count, box_offsets, freq_count, 1, tau_dev)
    folded_imag = folded_imag.reshape(shot_dev, trace_count, box_offsets, freq_count, 1, tau_dev)
    folded = jnp.concatenate([folded_real, folded_imag], axis=4).reshape(
        shot_dev, trace_count, box_offsets, freq_count, 2 * tau_dev
    )
    folded = jnp.transpose(folded, (3, 1, 0, 2, 4)).reshape(
        freq_count * trace_count, shot_dev * box_offsets, 2 * tau_dev
    )
    folded = lax.all_to_all(folded, ("freq", "trace"), split_axis=0, concat_axis=0, tiled=True)
    folded = folded.reshape(-1, 2 * tau_dev)
    sources = source_weights.reshape(-1, 2 * coeff_count)
    gram = jnp.einsum(
        "xk,xc->kc", sources, folded, precision=SPLIT, preferred_element_type=jnp.float32
    )
    coeff_real = gram[:coeff_count, :tau_dev] - gram[coeff_count:, tau_dev:]
    coeff_imag = gram[:coeff_count, tau_dev:] + gram[coeff_count:, :tau_dev]
    coeffs = jnp.concatenate([coeff_real, coeff_imag], axis=1)
    for level_no in range(level_weights.shape[0]):
        partner = from_partner(coeffs, "trace", level_no)
        weights = level_weights[level_no]
        stacked = jnp.concatenate([coeffs, partner], axis=0)
        real_rows = product(weights[:, : 2 * coeff_count], stacked)
        imag_rows = product(weights[:, 2 * coeff_count :], stacked)
        coeffs = jnp.concatenate(
            [
                real_rows[:, :tau_dev] - imag_rows[:, tau_dev:],
                real_rows[:, tau_dev:] + imag_rows[:, :tau_dev],
            ],
            axis=1,
        )
    image = product(slowness_weights[:, :coeff_count], coeffs[:, :tau_dev]) - product(
        slowness_weights[:, coeff_count:], coeffs[:, tau_dev:]
    )
    return lax.all_to_all(image, "freq", split_axis=0, concat_axis=1, tiled=True)


MESH = pl.DeviceIdType.MESH
CORES = 2


def halves(value):
    high = value.astype(jnp.bfloat16)
    low = (value - high.astype(jnp.float32)).astype(jnp.bfloat16)
    return high, low


def dot(left, right):
    return jnp.dot(left, right, preferred_element_type=jnp.float32)


def dot_pairs(left, right):
    return dot(left[0], right[0]) + (dot(left[0], right[1]) + dot(left[1], right[0]))


def exclusive_or(left, right, count):
    total, bit = 0, 1
    while bit < count:
        total = total + (left // bit + right // bit) % 2 * bit
        bit *= 2
    return total


def turned(real_rows, imag_rows, tau_dev):
    swapped = jnp.concatenate([-imag_rows[:, tau_dev:], imag_rows[:, :tau_dev]], axis=1)
    return real_rows + swapped


def kernel(
    freq_count, trace_count,
    x_hbm, s_hbm, w_hbm, e_hbm, table_hi_hbm, table_lo_hbm,
    out_ref,
    x_ref, s_ref, w_ref, e_ref, table_hi, table_lo,
    st_hi, st_lo, w_hi, w_lo, e_hi, e_lo,
    send, recv, acc, level_send, level_recv, image_send, image_recv,
    x_sems, load_sems, send_sems, recv_sems, level_ss, level_rs, image_ss, image_rs,
):
    fi, ti = lax.axis_index("freq"), lax.axis_index("trace")
    devices = freq_count * trace_count
    planes = trace_count // CORES
    me = fi * trace_count + ti
    my_plane, my_core = ti // CORES, ti % CORES
    shot_dev, offset_count, sample_count = x_ref.shape
    box_offsets = offset_count // trace_count
    coeff_count = w_ref.shape[1]
    tau_dev = TAUS // freq_count
    step = sample_count // (4 * TAUS)
    norm = 1.0 / math.sqrt(sample_count * FREQS)
    span = TAUS * step
    plane_offsets = CORES * box_offsets

    barrier = pltpu.get_barrier_semaphore()

    def greet(i, _):
        other = (me + i) % devices
        pl.semaphore_signal(
            barrier,
            inc=1,
            device_id={"freq": other // trace_count, "trace": other % trace_count},
            device_id_type=MESH,
        )
        return 0

    lax.fori_loop(1, devices, greet, 0)

    def plane_at(turn):
        return exclusive_or(my_plane, planes - 1 - turn, planes)

    def load_x(turn):
        rows = pl.ds(pl.multiple_of(plane_at(turn) * plane_offsets, plane_offsets), plane_offsets)
        return pltpu.make_async_copy(x_hbm.at[:, rows, :], x_ref.at[:, rows, :], x_sems.at[turn])

    loads = [
        pltpu.make_async_copy(source, target, load_sems.at[i])
        for i, (source, target) in enumerate(
            [
                (table_hi_hbm, table_hi),
                (table_lo_hbm, table_lo),
                (s_hbm, s_ref),
                (w_hbm, w_ref),
                (e_hbm, e_ref),
            ]
        )
    ]
    loads[0].start()
    load_x(0).start()
    loads[1].start()
    for turn in range(1, planes):
        load_x(turn).start()
    for load in loads[2:]:
        load.start()

    pick = (
        lax.broadcasted_iota(jnp.int32, (span, TAUS), 0)
        == lax.broadcasted_iota(jnp.int32, (span, TAUS), 1) * step
    ).astype(jnp.bfloat16)
    odd = lax.broadcasted_iota(jnp.int32, (1, sample_count), 1) % 2 == 1
    loads[0].wait()
    loads[1].wait()

    def block_copy(plane, f, core):
        return pltpu.make_async_remote_copy(
            src_ref=send.at[plane, f, core],
            dst_ref=recv.at[my_plane, fi, my_core],
            send_sem=send_sems.at[plane, f, core],
            recv_sem=recv_sems.at[my_plane, fi, my_core],
            device_id={"freq": f, "trace": plane * CORES + core},
            device_id_type=MESH,
        )

    def arrival(plane, f, core):
        return pltpu.make_async_remote_copy(
            src_ref=send.at[plane, f, core],
            dst_ref=recv.at[plane, f, core],
            send_sem=send_sems.at[plane, f, core],
            recv_sem=recv_sems.at[plane, f, core],
            device_id={"freq": f, "trace": plane * CORES + core},
            device_id_type=MESH,
        )

    def is_me(plane, f, core):
        return (f * trace_count + plane * CORES + core) == me

    def fold(turn, _):
        plane = plane_at(turn)
        load_x(turn).wait()
        rows = pl.ds(pl.multiple_of(plane * plane_offsets, plane_offsets), plane_offsets)
        samples = x_ref[:, rows, :].reshape(shot_dev * plane_offsets, sample_count)
        high, low = halves(samples)
        odd_sum = jnp.sum(jnp.where(odd, samples, 0.0), axis=1, keepdims=True) * norm
        imag = dot_pairs((high, low), (table_hi[...], table_lo[...]))
        real = (dot(high[:, :span], pick) + dot(low[:, :span], pick)) * (FREQS * norm) + odd_sum
        for f in range(freq_count):
            columns = slice(f * tau_dev, (f + 1) * tau_dev)
            block = jnp.concatenate([real[:, columns], imag[:, columns]], axis=1)
            block = block.reshape(shot_dev, CORES, box_offsets, 2 * tau_dev)
            for core in range(CORES):
                send[plane, f, core] = block[:, core]

        @pl.when(turn == 0)
        def _():
            pl.semaphore_wait(barrier, devices - 1)

        def start(i, _):
            f, core = (fi + i // CORES) % freq_count, i % CORES

            @pl.when(jnp.logical_not(is_me(plane, f, core)))
            def _():
                block_copy(plane, f, core).start()

            return 0

        lax.fori_loop(0, freq_count * CORES, start, 0)
        return 0

    lax.fori_loop(0, planes, fold, 0)
    recv[my_plane, fi, my_core] = send[my_plane, fi, my_core]

    loads[2].wait()
    pair_shots = CORES * shot_dev
    pair_rows = pair_shots * box_offsets

    def turn_sources(i, _):
        f, plane = i // planes, i % planes
        part = s_ref[pl.ds(i * pair_shots, pair_shots)].reshape(pair_rows, 2 * coeff_count)
        high, low = halves(part.T)
        columns = pl.ds(pl.multiple_of(f * pair_rows, pair_rows), pair_rows)
        st_hi[plane, :, columns] = high
        st_lo[plane, :, columns] = low
        return 0

    lax.fori_loop(0, freq_count * planes, turn_sources, 0)
    loads[3].wait()

    def split_level(level, _):
        w_hi[level], w_lo[level] = halves(w_ref[level])
        return 0

    lax.fori_loop(0, w_ref.shape[0], split_level, 0)
    loads[4].wait()
    e_hi[...], e_lo[...] = halves(e_ref[...])

    acc[...] = jnp.zeros_like(acc)

    def gram(turn, _):
        plane = exclusive_or(my_plane, turn, planes)

        def wait_for(i, _):
            f, core = i // CORES, i % CORES

            @pl.when(jnp.logical_not(is_me(plane, f, core)))
            def _():
                arrival(plane, f, core).wait_recv()

            return 0

        lax.fori_loop(0, freq_count * CORES, wait_for, 0)
        blocks = recv[plane].reshape(freq_count * pair_rows, 2 * tau_dev)
        acc[...] += dot_pairs((st_hi[plane], st_lo[plane]), halves(blocks))
        return 0

    lax.fori_loop(0, planes, gram, 0)
    coeffs = turned(acc[:coeff_count], acc[coeff_count:], tau_dev)

    for level in range(w_ref.shape[0]):
        level_send[level] = coeffs
        flip = 1 << level
        partner = ti + (1 - 2 * (ti // flip % 2)) * flip
        exchange = pltpu.make_async_remote_copy(
            src_ref=level_send.at[level],
            dst_ref=level_recv.at[level],
            send_sem=level_ss.at[level],
            recv_sem=level_rs.at[level],
            device_id={"freq": fi, "trace": partner},
            device_id_type=MESH,
        )
        exchange.start()

        def part(block, pairs):
            columns = slice(block * coeff_count, (block + 1) * coeff_count)
            return dot_pairs((w_hi[level, :, columns], w_lo[level, :, columns]), pairs)

        own = halves(coeffs)
        real_rows, imag_rows = part(0, own), part(2, own)
        exchange.wait()
        other = halves(level_recv[level])
        coeffs = turned(real_rows + part(1, other), imag_rows + part(3, other), tau_dev)

    pairs = halves(coeffs)
    image = (
        dot_pairs((e_hi[:, :coeff_count], e_lo[:, :coeff_count]), pairs)[:, :tau_dev]
        - dot_pairs((e_hi[:, coeff_count:], e_lo[:, coeff_count:]), pairs)[:, tau_dev:]
    )
    rows_out = out_ref.shape[0]
    for f in range(freq_count):
        image_send[f] = image[f * rows_out : (f + 1) * rows_out]

    def image_copy(target, source):
        return pltpu.make_async_remote_copy(
            src_ref=image_send.at[target],
            dst_ref=image_recv.at[source],
            send_sem=image_ss.at[target],
            recv_sem=image_rs.at[source],
            device_id={"freq": target, "trace": ti},
            device_id_type=MESH,
        )

    def start_image(i, _):
        image_copy((fi + i) % freq_count, fi).start()
        return 0

    def wait_image(i, _):
        other = (fi + i) % freq_count
        image_copy(other, fi).wait_send()
        image_copy(other, other).wait_recv()
        return 0

    lax.fori_loop(1, freq_count, start_image, 0)
    image_recv[fi] = image_send[fi]

    def wait_sent(i, _):
        plane, f, core = i // (freq_count * CORES), i // CORES % freq_count, i % CORES

        @pl.when(jnp.logical_not(is_me(plane, f, core)))
        def _():
            block_copy(plane, f, core).wait_send()

        return 0

    lax.fori_loop(0, devices, wait_sent, 0)
    lax.fori_loop(1, freq_count, wait_image, 0)
    out_ref[...] = jnp.concatenate([image_recv[f] for f in range(freq_count)], axis=1)


def fused(traces, source_weights, level_weights, slowness_weights):
    freq_count = lax.axis_size("freq")
    trace_count = lax.axis_size("trace")
    devices = freq_count * trace_count
    planes = trace_count // CORES
    shot_dev, offset_count, sample_count = traces.shape
    box_offsets = offset_count // trace_count
    columns = source_weights.shape[2]
    coeff_count = columns // 2
    levels = level_weights.shape[0]
    slow_dev = slowness_weights.shape[0]
    width = 2 * (TAUS // freq_count)
    table = imag_table(sample_count)
    table_hi = table.astype(jnp.bfloat16)
    table_lo = (table - table_hi.astype(np.float32)).astype(jnp.bfloat16)
    rows = freq_count * CORES * shot_dev * box_offsets
    blocks = (planes, freq_count, CORES)
    f32, bf16, dma = jnp.float32, jnp.bfloat16, pltpu.SemaphoreType.DMA
    rows_out = slow_dev // freq_count
    return pl.pallas_call(
        functools.partial(kernel, freq_count, trace_count),
        out_shape=jax.ShapeDtypeStruct((rows_out, TAUS), f32),
        in_specs=[pl.BlockSpec(memory_space=pl.ANY)] * 6,
        out_specs=pl.BlockSpec(memory_space=pltpu.VMEM),
        scratch_shapes=[
            pltpu.VMEM(traces.shape, f32),
            pltpu.VMEM(source_weights.shape, f32),
            pltpu.VMEM(level_weights.shape, f32),
            pltpu.VMEM(slowness_weights.shape, f32),
            pltpu.VMEM(table.shape, bf16),
            pltpu.VMEM(table.shape, bf16),
            pltpu.VMEM((planes, columns, rows), bf16),
            pltpu.VMEM((planes, columns, rows), bf16),
            pltpu.VMEM(level_weights.shape, bf16),
            pltpu.VMEM(level_weights.shape, bf16),
            pltpu.VMEM(slowness_weights.shape, bf16),
            pltpu.VMEM(slowness_weights.shape, bf16),
            pltpu.VMEM(blocks + (shot_dev, box_offsets, width), f32),
            pltpu.VMEM(blocks + (shot_dev, box_offsets, width), f32),
            pltpu.VMEM((columns, width), f32),
            pltpu.VMEM((levels, coeff_count, width), f32),
            pltpu.VMEM((levels, coeff_count, width), f32),
            pltpu.VMEM((freq_count, rows_out, width // 2), f32),
            pltpu.VMEM((freq_count, rows_out, width // 2), f32),
            dma((planes,)),
            dma((5,)),
            dma(blocks),
            dma(blocks),
            dma((levels,)),
            dma((levels,)),
            dma((freq_count,)),
            dma((freq_count,)),
        ],
        compiler_params=pltpu.CompilerParams(
            collective_id=0, has_side_effects=True, vmem_limit_bytes=60 * 1024 * 1024
        ),
        name="fold_and_butterfly",
    )(
        traces,
        source_weights,
        level_weights,
        slowness_weights,
        jnp.asarray(table_hi),
        jnp.asarray(table_lo),
    )


def solution(mesh):
    lanes = 2 * TAUS // mesh.shape["freq"]
    return jax.shard_map(
        fused if lanes % 128 == 0 else body,
        mesh=mesh,
        in_specs=(
            P(("freq", "trace"), None, None),
            P(None, "trace", None),
            P(None, "trace", None),
            P("trace", None),
        ),
        out_specs=P(("trace", "freq"), None),
        check_vma=False,
    )
```

```python
import functools
import math

import jax
import jax.numpy as jnp
import numpy as np
from jax import lax
from jax.experimental import pallas as pl
from jax.experimental.pallas import tpu as pltpu
from jax.sharding import PartitionSpec as P

FREQS = 1024
TAUS = 256


SPLIT = lax.Precision.HIGH


def from_partner(block, axis, apart):
    count = lax.axis_size(axis)
    route = []
    for low in range(count):
        high = low | 1 << apart
        if high != low and high < count:
            route += [(low, high), (high, low)]
    return lax.ppermute(block, axis, route)


def product(left, right):
    return jnp.dot(left, right, precision=SPLIT, preferred_element_type=jnp.float32)


def lag_series(sample_count):
    lags = np.arange(sample_count)
    turns = (np.arange(FREQS)[:, None] * lags[None, :]) % sample_count
    return np.exp(2j * np.pi * turns / sample_count).sum(axis=0)


def imag_table(sample_count):
    series = lag_series(sample_count).imag
    step = sample_count // (4 * TAUS)
    lags = (np.arange(TAUS)[None, :] * step - np.arange(sample_count)[:, None]) % sample_count
    return (series[lags] / math.sqrt(sample_count * FREQS)).astype(np.float32)


def body(traces, source_weights, level_weights, slowness_weights):
    freq_count = lax.axis_size("freq")
    trace_count = lax.axis_size("trace")
    shot_dev, offset_count, sample_count = traces.shape
    tau_dev = TAUS // freq_count
    box_offsets = offset_count // trace_count
    coeff_count = source_weights.shape[2] // 2
    step = sample_count // (4 * TAUS)
    norm = 1.0 / math.sqrt(sample_count * FREQS)
    samples = traces.reshape(-1, sample_count)
    odd = (jnp.arange(sample_count) % 2 == 1).astype(jnp.float32)
    odd_sum = jnp.sum(samples * odd, axis=1, keepdims=True) * norm
    span = TAUS * step
    pick = (jnp.arange(span)[:, None] == jnp.arange(TAUS)[None, :] * step).astype(jnp.float32)
    folded_real = product(samples[:, :span], pick) * (FREQS * norm) + odd_sum
    folded_imag = product(samples, jnp.asarray(imag_table(sample_count)))
    folded_real = folded_real.reshape(shot_dev, trace_count, box_offsets, freq_count, 1, tau_dev)
    folded_imag = folded_imag.reshape(shot_dev, trace_count, box_offsets, freq_count, 1, tau_dev)
    folded = jnp.concatenate([folded_real, folded_imag], axis=4).reshape(
        shot_dev, trace_count, box_offsets, freq_count, 2 * tau_dev
    )
    folded = jnp.transpose(folded, (3, 1, 0, 2, 4)).reshape(
        freq_count * trace_count, shot_dev * box_offsets, 2 * tau_dev
    )
    folded = lax.all_to_all(folded, ("freq", "trace"), split_axis=0, concat_axis=0, tiled=True)
    folded = folded.reshape(-1, 2 * tau_dev)
    sources = source_weights.reshape(-1, 2 * coeff_count)
    gram = jnp.einsum(
        "xk,xc->kc", sources, folded, precision=SPLIT, preferred_element_type=jnp.float32
    )
    coeff_real = gram[:coeff_count, :tau_dev] - gram[coeff_count:, tau_dev:]
    coeff_imag = gram[:coeff_count, tau_dev:] + gram[coeff_count:, :tau_dev]
    coeffs = jnp.concatenate([coeff_real, coeff_imag], axis=1)
    for level_no in range(level_weights.shape[0]):
        partner = from_partner(coeffs, "trace", level_no)
        weights = level_weights[level_no]
        stacked = jnp.concatenate([coeffs, partner], axis=0)
        real_rows = product(weights[:, : 2 * coeff_count], stacked)
        imag_rows = product(weights[:, 2 * coeff_count :], stacked)
        coeffs = jnp.concatenate(
            [
                real_rows[:, :tau_dev] - imag_rows[:, tau_dev:],
                real_rows[:, tau_dev:] + imag_rows[:, :tau_dev],
            ],
            axis=1,
        )
    image = product(slowness_weights[:, :coeff_count], coeffs[:, :tau_dev]) - product(
        slowness_weights[:, coeff_count:], coeffs[:, tau_dev:]
    )
    return lax.all_to_all(image, "freq", split_axis=0, concat_axis=1, tiled=True)


MESH = pl.DeviceIdType.MESH
CORES = 2


def halves(value):
    high = value.astype(jnp.bfloat16)
    low = (value - high.astype(jnp.float32)).astype(jnp.bfloat16)
    return high, low


def dot(left, right):
    return jnp.dot(left, right, preferred_element_type=jnp.float32)


def dot_pairs(left, right):
    return dot(left[0], right[0]) + (dot(left[0], right[1]) + dot(left[1], right[0]))


def exclusive_or(left, right, count):
    total, bit = 0, 1
    while bit < count:
        total = total + (left // bit + right // bit) % 2 * bit
        bit *= 2
    return total


def turned(real_rows, imag_rows, tau_dev):
    swapped = jnp.concatenate([-imag_rows[:, tau_dev:], imag_rows[:, :tau_dev]], axis=1)
    return real_rows + swapped


def kernel(
    freq_count, trace_count,
    x_hbm, s_hbm, w_hbm, e_hbm, table_hi_hbm, table_lo_hbm,
    out_ref,
    x_ref, s_ref, w_ref, e_ref, table_hi, table_lo,
    st_hi, st_lo, w_hi, w_lo, e_hi, e_lo,
    send, recv, acc, level_send, level_recv, image_send, image_recv,
    x_sems, load_sems, send_sems, recv_sems, level_ss, level_rs, image_ss, image_rs,
):
    fi, ti = lax.axis_index("freq"), lax.axis_index("trace")
    devices = freq_count * trace_count
    planes = trace_count // CORES
    me = fi * trace_count + ti
    my_plane, my_core = ti // CORES, ti % CORES
    shot_dev, offset_count, sample_count = x_ref.shape
    box_offsets = offset_count // trace_count
    coeff_count = w_ref.shape[1]
    tau_dev = TAUS // freq_count
    step = sample_count // (4 * TAUS)
    norm = 1.0 / math.sqrt(sample_count * FREQS)
    span = TAUS * step
    plane_offsets = CORES * box_offsets

    barrier = pltpu.get_barrier_semaphore()

    def greet(i, _):
        other = (me + i) % devices
        pl.semaphore_signal(
            barrier,
            inc=1,
            device_id={"freq": other // trace_count, "trace": other % trace_count},
            device_id_type=MESH,
        )
        return 0

    lax.fori_loop(1, devices, greet, 0)

    def plane_at(turn):
        return exclusive_or(my_plane, planes - 1 - turn, planes)

    def load_x(turn):
        rows = pl.ds(pl.multiple_of(plane_at(turn) * plane_offsets, plane_offsets), plane_offsets)
        return pltpu.make_async_copy(x_hbm.at[:, rows, :], x_ref.at[:, rows, :], x_sems.at[turn])

    loads = [
        pltpu.make_async_copy(source, target, load_sems.at[i])
        for i, (source, target) in enumerate(
            [
                (table_hi_hbm, table_hi),
                (table_lo_hbm, table_lo),
                (s_hbm, s_ref),
                (w_hbm, w_ref),
                (e_hbm, e_ref),
            ]
        )
    ]
    loads[0].start()
    load_x(0).start()
    loads[1].start()
    for turn in range(1, planes):
        load_x(turn).start()
    for load in loads[2:]:
        load.start()

    pick = (
        lax.broadcasted_iota(jnp.int32, (span, TAUS), 0)
        == lax.broadcasted_iota(jnp.int32, (span, TAUS), 1) * step
    ).astype(jnp.bfloat16)
    odd = lax.broadcasted_iota(jnp.int32, (1, sample_count), 1) % 2 == 1
    loads[0].wait()
    loads[1].wait()

    def block_copy(plane, f, core):
        return pltpu.make_async_remote_copy(
            src_ref=send.at[plane, f, core],
            dst_ref=recv.at[my_plane, fi, my_core],
            send_sem=send_sems.at[plane, f, core],
            recv_sem=recv_sems.at[my_plane, fi, my_core],
            device_id={"freq": f, "trace": plane * CORES + core},
            device_id_type=MESH,
        )

    def arrival(plane, f, core):
        return pltpu.make_async_remote_copy(
            src_ref=send.at[plane, f, core],
            dst_ref=recv.at[plane, f, core],
            send_sem=send_sems.at[plane, f, core],
            recv_sem=recv_sems.at[plane, f, core],
            device_id={"freq": f, "trace": plane * CORES + core},
            device_id_type=MESH,
        )

    def is_me(plane, f, core):
        return (f * trace_count + plane * CORES + core) == me

    def fold(turn, _):
        plane = plane_at(turn)
        load_x(turn).wait()
        rows = pl.ds(pl.multiple_of(plane * plane_offsets, plane_offsets), plane_offsets)
        samples = x_ref[:, rows, :].reshape(shot_dev * plane_offsets, sample_count)
        high, low = halves(samples)
        odd_sum = jnp.sum(jnp.where(odd, samples, 0.0), axis=1, keepdims=True) * norm
        imag = dot_pairs((high, low), (table_hi[...], table_lo[...]))
        real = (dot(high[:, :span], pick) + dot(low[:, :span], pick)) * (FREQS * norm) + odd_sum
        for f in range(freq_count):
            columns = slice(f * tau_dev, (f + 1) * tau_dev)
            block = jnp.concatenate([real[:, columns], imag[:, columns]], axis=1)
            block = block.reshape(shot_dev, CORES, box_offsets, 2 * tau_dev)
            for core in range(CORES):
                send[plane, f, core] = block[:, core]

        @pl.when(turn == 0)
        def _():
            pl.semaphore_wait(barrier, devices - 1)

        def start(i, _):
            f, core = (fi + i // CORES) % freq_count, i % CORES

            @pl.when(jnp.logical_not(is_me(plane, f, core)))
            def _():
                block_copy(plane, f, core).start()

            return 0

        lax.fori_loop(0, freq_count * CORES, start, 0)
        return 0

    lax.fori_loop(0, planes, fold, 0)
    recv[my_plane, fi, my_core] = send[my_plane, fi, my_core]

    loads[2].wait()
    pair_shots = CORES * shot_dev
    pair_rows = pair_shots * box_offsets

    def turn_sources(i, _):
        f, plane = i // planes, i % planes
        part = s_ref[pl.ds(i * pair_shots, pair_shots)].reshape(pair_rows, 2 * coeff_count)
        high, low = halves(part.T)
        columns = pl.ds(pl.multiple_of(f * pair_rows, pair_rows), pair_rows)
        st_hi[plane, :, columns] = high
        st_lo[plane, :, columns] = low
        return 0

    lax.fori_loop(0, freq_count * planes, turn_sources, 0)
    loads[3].wait()

    def split_level(level, _):
        w_hi[level], w_lo[level] = halves(w_ref[level])
        return 0

    lax.fori_loop(0, w_ref.shape[0], split_level, 0)
    loads[4].wait()
    e_hi[...], e_lo[...] = halves(e_ref[...])

    acc[...] = jnp.zeros_like(acc)

    def gram(turn, _):
        plane = exclusive_or(my_plane, turn, planes)

        def wait_for(i, _):
            f, core = i // CORES, i % CORES

            @pl.when(jnp.logical_not(is_me(plane, f, core)))
            def _():
                arrival(plane, f, core).wait_recv()

            return 0

        lax.fori_loop(0, freq_count * CORES, wait_for, 0)
        blocks = recv[plane].reshape(freq_count * pair_rows, 2 * tau_dev)
        acc[...] += dot_pairs((st_hi[plane], st_lo[plane]), halves(blocks))
        return 0

    lax.fori_loop(0, planes, gram, 0)
    level_send[0] = turned(acc[:coeff_count], acc[coeff_count:], tau_dev)

    def apply_level(level, flip):
        partner = ti + (1 - 2 * (ti // flip % 2)) * flip
        exchange = pltpu.make_async_remote_copy(
            src_ref=level_send.at[level],
            dst_ref=level_recv.at[level],
            send_sem=level_ss.at[level],
            recv_sem=level_rs.at[level],
            device_id={"freq": fi, "trace": partner},
            device_id_type=MESH,
        )
        exchange.start()

        def part(block, pairs):
            columns = slice(block * coeff_count, (block + 1) * coeff_count)
            return dot_pairs((w_hi[level, :, columns], w_lo[level, :, columns]), pairs)

        own = halves(level_send[level])
        real_rows, imag_rows = part(0, own), part(2, own)
        exchange.wait()
        other = halves(level_recv[level])
        level_send[level + 1] = turned(
            real_rows + part(1, other), imag_rows + part(3, other), tau_dev
        )
        return 2 * flip

    levels = w_ref.shape[0]
    lax.fori_loop(0, levels, apply_level, 1)
    pairs = halves(level_send[levels])
    image = (
        dot_pairs((e_hi[:, :coeff_count], e_lo[:, :coeff_count]), pairs)[:, :tau_dev]
        - dot_pairs((e_hi[:, coeff_count:], e_lo[:, coeff_count:]), pairs)[:, tau_dev:]
    )
    rows_out = out_ref.shape[0]
    for f in range(freq_count):
        top = f * rows_out
        middle, bottom = top + rows_out // 2, top + rows_out
        image_send[f] = jnp.concatenate([image[top:middle], image[middle:bottom]], axis=1)

    def image_copy(target, source):
        return pltpu.make_async_remote_copy(
            src_ref=image_send.at[target],
            dst_ref=image_recv.at[source],
            send_sem=image_ss.at[target],
            recv_sem=image_rs.at[source],
            device_id={"freq": target, "trace": ti},
            device_id_type=MESH,
        )

    def start_image(i, _):
        image_copy((fi + i) % freq_count, fi).start()
        return 0

    def wait_image(i, _):
        other = (fi + i) % freq_count
        image_copy(other, fi).wait_send()
        image_copy(other, other).wait_recv()
        return 0

    lax.fori_loop(1, freq_count, start_image, 0)
    image_recv[fi] = image_send[fi]

    def wait_sent(i, _):
        plane, f, core = i // (freq_count * CORES), i // CORES % freq_count, i % CORES

        @pl.when(jnp.logical_not(is_me(plane, f, core)))
        def _():
            block_copy(plane, f, core).wait_send()

        return 0

    lax.fori_loop(0, devices, wait_sent, 0)
    lax.fori_loop(1, freq_count, wait_image, 0)
    for part in range(2):
        out_ref[part * rows_out // 2 : (part + 1) * rows_out // 2] = jnp.concatenate(
            [image_recv[f, :, part * tau_dev : (part + 1) * tau_dev] for f in range(freq_count)],
            axis=1,
        )


def fused(traces, source_weights, level_weights, slowness_weights):
    freq_count = lax.axis_size("freq")
    trace_count = lax.axis_size("trace")
    devices = freq_count * trace_count
    planes = trace_count // CORES
    shot_dev, offset_count, sample_count = traces.shape
    box_offsets = offset_count // trace_count
    columns = source_weights.shape[2]
    coeff_count = columns // 2
    levels = level_weights.shape[0]
    slow_dev = slowness_weights.shape[0]
    width = 2 * (TAUS // freq_count)
    table = imag_table(sample_count)
    table_hi = table.astype(jnp.bfloat16)
    table_lo = (table - table_hi.astype(np.float32)).astype(jnp.bfloat16)
    rows = freq_count * CORES * shot_dev * box_offsets
    blocks = (planes, freq_count, CORES)
    f32, bf16, dma = jnp.float32, jnp.bfloat16, pltpu.SemaphoreType.DMA
    rows_out = slow_dev // freq_count
    return pl.pallas_call(
        functools.partial(kernel, freq_count, trace_count),
        out_shape=jax.ShapeDtypeStruct((rows_out, TAUS), f32),
        in_specs=[pl.BlockSpec(memory_space=pl.ANY)] * 6,
        out_specs=pl.BlockSpec(memory_space=pltpu.VMEM),
        scratch_shapes=[
            pltpu.VMEM(traces.shape, f32),
            pltpu.VMEM(source_weights.shape, f32),
            pltpu.VMEM(level_weights.shape, f32),
            pltpu.VMEM(slowness_weights.shape, f32),
            pltpu.VMEM(table.shape, bf16),
            pltpu.VMEM(table.shape, bf16),
            pltpu.VMEM((planes, columns, rows), bf16),
            pltpu.VMEM((planes, columns, rows), bf16),
            pltpu.VMEM(level_weights.shape, bf16),
            pltpu.VMEM(level_weights.shape, bf16),
            pltpu.VMEM(slowness_weights.shape, bf16),
            pltpu.VMEM(slowness_weights.shape, bf16),
            pltpu.VMEM(blocks + (shot_dev, box_offsets, width), f32),
            pltpu.VMEM(blocks + (shot_dev, box_offsets, width), f32),
            pltpu.VMEM((columns, width), f32),
            pltpu.VMEM((levels + 1, coeff_count, width), f32),
            pltpu.VMEM((levels, coeff_count, width), f32),
            pltpu.VMEM((freq_count, rows_out // 2, width), f32),
            pltpu.VMEM((freq_count, rows_out // 2, width), f32),
            dma((planes,)),
            dma((5,)),
            dma(blocks),
            dma(blocks),
            dma((levels,)),
            dma((levels,)),
            dma((freq_count,)),
            dma((freq_count,)),
        ],
        compiler_params=pltpu.CompilerParams(
            collective_id=0, has_side_effects=True, vmem_limit_bytes=60 * 1024 * 1024
        ),
        name="fold_and_butterfly",
    )(
        traces,
        source_weights,
        level_weights,
        slowness_weights,
        jnp.asarray(table_hi),
        jnp.asarray(table_lo),
    )


def solution(mesh):
    lanes = 2 * TAUS // mesh.shape["freq"]
    return jax.shard_map(
        fused if lanes % 128 == 0 else body,
        mesh=mesh,
        in_specs=(
            P(("freq", "trace"), None, None),
            P(None, "trace", None),
            P(None, "trace", None),
            P("trace", None),
        ),
        out_specs=P(("trace", "freq"), None),
        check_vma=False,
    )
```

```python
import functools
import math

import jax
import jax.numpy as jnp
import numpy as np
from jax import lax
from jax.experimental import pallas as pl
from jax.experimental.pallas import tpu as pltpu
from jax.sharding import PartitionSpec as P

FREQS = 1024
TAUS = 256


SPLIT = lax.Precision.HIGH


def from_partner(block, axis, apart):
    count = lax.axis_size(axis)
    route = []
    for low in range(count):
        high = low | 1 << apart
        if high != low and high < count:
            route += [(low, high), (high, low)]
    return lax.ppermute(block, axis, route)


def product(left, right):
    return jnp.dot(left, right, precision=SPLIT, preferred_element_type=jnp.float32)


def lag_series(sample_count):
    lags = np.arange(sample_count)
    turns = (np.arange(FREQS)[:, None] * lags[None, :]) % sample_count
    return np.exp(2j * np.pi * turns / sample_count).sum(axis=0)


def imag_table(sample_count):
    series = lag_series(sample_count).imag
    step = sample_count // (4 * TAUS)
    lags = (np.arange(TAUS)[None, :] * step - np.arange(sample_count)[:, None]) % sample_count
    return (series[lags] / math.sqrt(sample_count * FREQS)).astype(np.float32)


def body(traces, source_weights, level_weights, slowness_weights):
    freq_count = lax.axis_size("freq")
    trace_count = lax.axis_size("trace")
    shot_dev, offset_count, sample_count = traces.shape
    tau_dev = TAUS // freq_count
    box_offsets = offset_count // trace_count
    coeff_count = source_weights.shape[2] // 2
    step = sample_count // (4 * TAUS)
    norm = 1.0 / math.sqrt(sample_count * FREQS)
    samples = traces.reshape(-1, sample_count)
    odd = (jnp.arange(sample_count) % 2 == 1).astype(jnp.float32)
    odd_sum = jnp.sum(samples * odd, axis=1, keepdims=True) * norm
    span = TAUS * step
    pick = (jnp.arange(span)[:, None] == jnp.arange(TAUS)[None, :] * step).astype(jnp.float32)
    folded_real = product(samples[:, :span], pick) * (FREQS * norm) + odd_sum
    folded_imag = product(samples, jnp.asarray(imag_table(sample_count)))
    folded_real = folded_real.reshape(shot_dev, trace_count, box_offsets, freq_count, 1, tau_dev)
    folded_imag = folded_imag.reshape(shot_dev, trace_count, box_offsets, freq_count, 1, tau_dev)
    folded = jnp.concatenate([folded_real, folded_imag], axis=4).reshape(
        shot_dev, trace_count, box_offsets, freq_count, 2 * tau_dev
    )
    folded = jnp.transpose(folded, (3, 1, 0, 2, 4)).reshape(
        freq_count * trace_count, shot_dev * box_offsets, 2 * tau_dev
    )
    folded = lax.all_to_all(folded, ("freq", "trace"), split_axis=0, concat_axis=0, tiled=True)
    folded = folded.reshape(-1, 2 * tau_dev)
    sources = source_weights.reshape(-1, 2 * coeff_count)
    gram = jnp.einsum(
        "xk,xc->kc", sources, folded, precision=SPLIT, preferred_element_type=jnp.float32
    )
    coeff_real = gram[:coeff_count, :tau_dev] - gram[coeff_count:, tau_dev:]
    coeff_imag = gram[:coeff_count, tau_dev:] + gram[coeff_count:, :tau_dev]
    coeffs = jnp.concatenate([coeff_real, coeff_imag], axis=1)
    for level_no in range(level_weights.shape[0]):
        partner = from_partner(coeffs, "trace", level_no)
        weights = level_weights[level_no]
        stacked = jnp.concatenate([coeffs, partner], axis=0)
        real_rows = product(weights[:, : 2 * coeff_count], stacked)
        imag_rows = product(weights[:, 2 * coeff_count :], stacked)
        coeffs = jnp.concatenate(
            [
                real_rows[:, :tau_dev] - imag_rows[:, tau_dev:],
                real_rows[:, tau_dev:] + imag_rows[:, :tau_dev],
            ],
            axis=1,
        )
    image = product(slowness_weights[:, :coeff_count], coeffs[:, :tau_dev]) - product(
        slowness_weights[:, coeff_count:], coeffs[:, tau_dev:]
    )
    return lax.all_to_all(image, "freq", split_axis=0, concat_axis=1, tiled=True)


MESH = pl.DeviceIdType.MESH
CORES = 2


def halves(value):
    high = value.astype(jnp.bfloat16)
    low = (value - high.astype(jnp.float32)).astype(jnp.bfloat16)
    return high, low


def dot(left, right):
    return jnp.dot(left, right, preferred_element_type=jnp.float32)


def dot_pairs(left, right):
    return dot(left[0], right[0]) + (dot(left[0], right[1]) + dot(left[1], right[0]))


def exclusive_or(left, right, count):
    total, bit = 0, 1
    while bit < count:
        total = total + (left // bit + right // bit) % 2 * bit
        bit *= 2
    return total


def turned(real_rows, imag_rows, tau_dev):
    swapped = jnp.concatenate([-imag_rows[:, tau_dev:], imag_rows[:, :tau_dev]], axis=1)
    return real_rows + swapped


def kernel(
    freq_count, trace_count,
    x_hbm, s_hbm, w_hbm, e_hbm, table_hi_hbm, table_lo_hbm,
    out_ref,
    x_ref, s_ref, w_ref, e_ref, table_hi, table_lo,
    st_hi, st_lo, w_hi, w_lo, e_hi, e_lo,
    send, recv, acc, level_send, level_recv, image_send, image_recv,
    x_sems, load_sems, send_sems, recv_sems, level_ss, level_rs, image_ss, image_rs,
):
    fi, ti = lax.axis_index("freq"), lax.axis_index("trace")
    devices = freq_count * trace_count
    planes = trace_count // CORES
    me = fi * trace_count + ti
    my_plane, my_core = ti // CORES, ti % CORES
    shot_dev, offset_count, sample_count = x_ref.shape
    box_offsets = offset_count // trace_count
    coeff_count = w_ref.shape[1]
    tau_dev = TAUS // freq_count
    step = sample_count // (4 * TAUS)
    norm = 1.0 / math.sqrt(sample_count * FREQS)
    span = TAUS * step
    plane_offsets = CORES * box_offsets

    barrier = pltpu.get_barrier_semaphore()

    def greet(i, _):
        other = (me + i) % devices
        pl.semaphore_signal(
            barrier,
            inc=1,
            device_id={"freq": other // trace_count, "trace": other % trace_count},
            device_id_type=MESH,
        )
        return 0

    lax.fori_loop(1, devices, greet, 0)

    def plane_at(turn):
        return exclusive_or(my_plane, (planes - 1 - turn) // 2 * 2 + turn % 2, planes)

    def load_x(turn):
        rows = pl.ds(pl.multiple_of(plane_at(turn) * plane_offsets, plane_offsets), plane_offsets)
        return pltpu.make_async_copy(x_hbm.at[:, rows, :], x_ref.at[:, rows, :], x_sems.at[turn])

    loads = [
        pltpu.make_async_copy(source, target, load_sems.at[i])
        for i, (source, target) in enumerate(
            [
                (table_hi_hbm, table_hi),
                (table_lo_hbm, table_lo),
                (s_hbm, s_ref),
                (w_hbm, w_ref),
                (e_hbm, e_ref),
            ]
        )
    ]
    loads[0].start()
    load_x(0).start()
    loads[1].start()
    for turn in range(1, planes):
        load_x(turn).start()
    for load in loads[2:]:
        load.start()

    pick = (
        lax.broadcasted_iota(jnp.int32, (span, TAUS), 0)
        == lax.broadcasted_iota(jnp.int32, (span, TAUS), 1) * step
    ).astype(jnp.bfloat16)
    odd = lax.broadcasted_iota(jnp.int32, (1, sample_count), 1) % 2 == 1
    loads[0].wait()
    loads[1].wait()

    def block_copy(plane, f, core):
        return pltpu.make_async_remote_copy(
            src_ref=send.at[plane, f, core],
            dst_ref=recv.at[my_plane, fi, my_core],
            send_sem=send_sems.at[plane, f, core],
            recv_sem=recv_sems.at[my_plane, fi, my_core],
            device_id={"freq": f, "trace": plane * CORES + core},
            device_id_type=MESH,
        )

    def arrival(plane, f, core):
        return pltpu.make_async_remote_copy(
            src_ref=send.at[plane, f, core],
            dst_ref=recv.at[plane, f, core],
            send_sem=send_sems.at[plane, f, core],
            recv_sem=recv_sems.at[plane, f, core],
            device_id={"freq": f, "trace": plane * CORES + core},
            device_id_type=MESH,
        )

    def is_me(plane, f, core):
        return (f * trace_count + plane * CORES + core) == me

    def fold(turn, _):
        plane = plane_at(turn)
        load_x(turn).wait()
        rows = pl.ds(pl.multiple_of(plane * plane_offsets, plane_offsets), plane_offsets)
        samples = x_ref[:, rows, :].reshape(shot_dev * plane_offsets, sample_count)
        high, low = halves(samples)
        odd_sum = jnp.sum(jnp.where(odd, samples, 0.0), axis=1, keepdims=True) * norm
        imag = dot_pairs((high, low), (table_hi[...], table_lo[...]))
        real = (dot(high[:, :span], pick) + dot(low[:, :span], pick)) * (FREQS * norm) + odd_sum
        for f in range(freq_count):
            columns = slice(f * tau_dev, (f + 1) * tau_dev)
            block = jnp.concatenate([real[:, columns], imag[:, columns]], axis=1)
            block = block.reshape(shot_dev, CORES, box_offsets, 2 * tau_dev)
            for core in range(CORES):
                send[plane, f, core] = block[:, core]

        @pl.when(turn == 0)
        def _():
            pl.semaphore_wait(barrier, devices - 1)

        def start(i, _):
            f, core = exclusive_or(fi, freq_count - 1 - i // CORES, freq_count), i % CORES

            @pl.when(jnp.logical_not(is_me(plane, f, core)))
            def _():
                block_copy(plane, f, core).start()

            return 0

        lax.fori_loop(0, freq_count * CORES, start, 0)
        return 0

    lax.fori_loop(0, planes, fold, 0)
    recv[my_plane, fi, my_core] = send[my_plane, fi, my_core]

    loads[2].wait()
    pair_shots = CORES * shot_dev
    pair_rows = pair_shots * box_offsets

    def turn_sources(i, _):
        f, plane = i // planes, i % planes
        part = s_ref[pl.ds(i * pair_shots, pair_shots)].reshape(pair_rows, 2 * coeff_count)
        high, low = halves(part.T)
        columns = pl.ds(pl.multiple_of(f * pair_rows, pair_rows), pair_rows)
        st_hi[plane, :, columns] = high
        st_lo[plane, :, columns] = low
        return 0

    lax.fori_loop(0, freq_count * planes, turn_sources, 0)
    loads[3].wait()

    def split_level(level, _):
        w_hi[level], w_lo[level] = halves(w_ref[level])
        return 0

    lax.fori_loop(0, w_ref.shape[0], split_level, 0)
    loads[4].wait()
    e_hi[...], e_lo[...] = halves(e_ref[...])

    acc[...] = jnp.zeros_like(acc)

    def gram(turn, _):
        plane = exclusive_or(my_plane, turn, planes)

        def wait_for(i, _):
            f, core = i // CORES, i % CORES

            @pl.when(jnp.logical_not(is_me(plane, f, core)))
            def _():
                arrival(plane, f, core).wait_recv()

            return 0

        lax.fori_loop(0, freq_count * CORES, wait_for, 0)
        blocks = recv[plane].reshape(freq_count * pair_rows, 2 * tau_dev)
        acc[...] += dot_pairs((st_hi[plane], st_lo[plane]), halves(blocks))
        return 0

    lax.fori_loop(0, planes, gram, 0)
    level_send[0] = turned(acc[:coeff_count], acc[coeff_count:], tau_dev)

    def apply_level(level, flip):
        partner = ti + (1 - 2 * (ti // flip % 2)) * flip
        exchange = pltpu.make_async_remote_copy(
            src_ref=level_send.at[level],
            dst_ref=level_recv.at[level],
            send_sem=level_ss.at[level],
            recv_sem=level_rs.at[level],
            device_id={"freq": fi, "trace": partner},
            device_id_type=MESH,
        )
        exchange.start()

        def part(block, pairs):
            columns = slice(block * coeff_count, (block + 1) * coeff_count)
            return dot_pairs((w_hi[level, :, columns], w_lo[level, :, columns]), pairs)

        own = halves(level_send[level])
        real_rows, imag_rows = part(0, own), part(2, own)
        exchange.wait()
        other = halves(level_recv[level])
        level_send[level + 1] = turned(
            real_rows + part(1, other), imag_rows + part(3, other), tau_dev
        )
        return 2 * flip

    levels = w_ref.shape[0]
    lax.fori_loop(0, levels, apply_level, 1)
    pairs = halves(level_send[levels])
    image = (
        dot_pairs((e_hi[:, :coeff_count], e_lo[:, :coeff_count]), pairs)[:, :tau_dev]
        - dot_pairs((e_hi[:, coeff_count:], e_lo[:, coeff_count:]), pairs)[:, tau_dev:]
    )
    rows_out = out_ref.shape[0]
    for f in range(freq_count):
        top = f * rows_out
        middle, bottom = top + rows_out // 2, top + rows_out
        image_send[f] = jnp.concatenate([image[top:middle], image[middle:bottom]], axis=1)

    def image_copy(target, source):
        return pltpu.make_async_remote_copy(
            src_ref=image_send.at[target],
            dst_ref=image_recv.at[source],
            send_sem=image_ss.at[target],
            recv_sem=image_rs.at[source],
            device_id={"freq": target, "trace": ti},
            device_id_type=MESH,
        )

    def start_image(i, _):
        image_copy((fi + i) % freq_count, fi).start()
        return 0

    def wait_image(i, _):
        other = (fi + i) % freq_count
        image_copy(other, fi).wait_send()
        image_copy(other, other).wait_recv()
        return 0

    lax.fori_loop(1, freq_count, start_image, 0)
    image_recv[fi] = image_send[fi]

    def wait_sent(i, _):
        plane, f, core = i // (freq_count * CORES), i // CORES % freq_count, i % CORES

        @pl.when(jnp.logical_not(is_me(plane, f, core)))
        def _():
            block_copy(plane, f, core).wait_send()

        return 0

    lax.fori_loop(0, devices, wait_sent, 0)
    lax.fori_loop(1, freq_count, wait_image, 0)
    for part in range(2):
        out_ref[part * rows_out // 2 : (part + 1) * rows_out // 2] = jnp.concatenate(
            [image_recv[f, :, part * tau_dev : (part + 1) * tau_dev] for f in range(freq_count)],
            axis=1,
        )


def fused(traces, source_weights, level_weights, slowness_weights):
    freq_count = lax.axis_size("freq")
    trace_count = lax.axis_size("trace")
    devices = freq_count * trace_count
    planes = trace_count // CORES
    shot_dev, offset_count, sample_count = traces.shape
    box_offsets = offset_count // trace_count
    columns = source_weights.shape[2]
    coeff_count = columns // 2
    levels = level_weights.shape[0]
    slow_dev = slowness_weights.shape[0]
    width = 2 * (TAUS // freq_count)
    table = imag_table(sample_count)
    table_hi = table.astype(jnp.bfloat16)
    table_lo = (table - table_hi.astype(np.float32)).astype(jnp.bfloat16)
    rows = freq_count * CORES * shot_dev * box_offsets
    blocks = (planes, freq_count, CORES)
    f32, bf16, dma = jnp.float32, jnp.bfloat16, pltpu.SemaphoreType.DMA
    rows_out = slow_dev // freq_count
    return pl.pallas_call(
        functools.partial(kernel, freq_count, trace_count),
        out_shape=jax.ShapeDtypeStruct((rows_out, TAUS), f32),
        in_specs=[pl.BlockSpec(memory_space=pl.ANY)] * 6,
        out_specs=pl.BlockSpec(memory_space=pltpu.VMEM),
        scratch_shapes=[
            pltpu.VMEM(traces.shape, f32),
            pltpu.VMEM(source_weights.shape, f32),
            pltpu.VMEM(level_weights.shape, f32),
            pltpu.VMEM(slowness_weights.shape, f32),
            pltpu.VMEM(table.shape, bf16),
            pltpu.VMEM(table.shape, bf16),
            pltpu.VMEM((planes, columns, rows), bf16),
            pltpu.VMEM((planes, columns, rows), bf16),
            pltpu.VMEM(level_weights.shape, bf16),
            pltpu.VMEM(level_weights.shape, bf16),
            pltpu.VMEM(slowness_weights.shape, bf16),
            pltpu.VMEM(slowness_weights.shape, bf16),
            pltpu.VMEM(blocks + (shot_dev, box_offsets, width), f32),
            pltpu.VMEM(blocks + (shot_dev, box_offsets, width), f32),
            pltpu.VMEM((columns, width), f32),
            pltpu.VMEM((levels + 1, coeff_count, width), f32),
            pltpu.VMEM((levels, coeff_count, width), f32),
            pltpu.VMEM((freq_count, rows_out // 2, width), f32),
            pltpu.VMEM((freq_count, rows_out // 2, width), f32),
            dma((planes,)),
            dma((5,)),
            dma(blocks),
            dma(blocks),
            dma((levels,)),
            dma((levels,)),
            dma((freq_count,)),
            dma((freq_count,)),
        ],
        compiler_params=pltpu.CompilerParams(
            collective_id=0, has_side_effects=True, vmem_limit_bytes=60 * 1024 * 1024
        ),
        name="fold_and_butterfly",
    )(
        traces,
        source_weights,
        level_weights,
        slowness_weights,
        jnp.asarray(table_hi),
        jnp.asarray(table_lo),
    )


def solution(mesh):
    lanes = 2 * TAUS // mesh.shape["freq"]
    return jax.shard_map(
        fused if lanes % 128 == 0 else body,
        mesh=mesh,
        in_specs=(
            P(("freq", "trace"), None, None),
            P(None, "trace", None),
            P(None, "trace", None),
            P("trace", None),
        ),
        out_specs=P(("trace", "freq"), None),
        check_vma=False,
    )
```
